32 devices in a mesh: grp: 2 (over y), slc: 4 (over z), coil: 2 (over x), vol: 2 (over core).
Axes of the slice: x: 2, y: 2, z: 4, core: 2. Of those that a mesh axis runs over, the one named last changes fastest.
Arguments:
- images: bfloat16 [4, 32, 2, 220, 220], P(('grp', 'vol'), 'slc'), parts along dimension 0, may hold values from -6 to 6
- coil_maps: bfloat16 [8, 32, 2, 220, 220], P(('grp', 'coil'), 'slc'), parts along dimension 0, may hold values from -3 to 3
- kspace: bfloat16 [4, 4, 4, 2, 220, 220], P(('grp', 'vol'), 'slc', 'coil'), parts along dimension 0, may hold values from -12 to 12
- shift_index: int32 [32], P('slc'), may hold values from 0 to 7
- phase_offset: float32 [32, 220], P('slc'), may hold values from -3.140625 to 3.140625
- group_order: int32 [4], replicated, may hold values from 0 to 3, each once
Outputs:
- grad_phase: float32 [64, 220], P(('grp', 'slc')), parts along dimension 0
The draws below stay inside these ranges and needn't reach their ends.
There are 2 independent parts, one for each index of `grp`. The reference program is written for one: setup_inputs(seed, part) draws one part's arguments, and reference() takes and returns one part's arrays. A program takes and returns all parts, laid end to end along the dimension named above; an argument that names none is the same for every part. Nothing has to cross between parts.
Inputs may be any that keep to these rules, and one draw needn't show every extreme that they name: group_order names each of the 4 measured rows exactly once.
All inputs are finite; a program needn't handle non-finite values.
Results may differ from the reference program's by a relative error of at most 0.0096.
Values may be sent and summed in bfloat16 or wider, within the bound.
A program may use at most 64 MiB of HBM per device.

```python
import math
import jax
import jax.numpy as jnp
from jax import lax

MATRIX = 220
MB = 8
COILS = 4
VOLS = 2
SLICES = 32
GROUPS = 4


def set_ends(drawn, key, low, largest):
    extent = drawn.shape
    place = [jax.random.randint(jax.random.fold_in(key, axis), (), 0, extent[axis]) for axis in range(len(extent))]
    drawn = drawn.at[tuple(place)].set(low)
    longest = extent.index(max(extent))
    place[longest] = (place[longest] + 1) % extent[longest]
    return drawn.at[tuple(place)].set(largest)


def level_of(rng, extent, split, low, largest):
    factor_of, own = 1.0, jax.random.fold_in(rng, 6)
    for position, blocks in split:
        steps = jnp.exp(jax.random.uniform(jax.random.fold_in(own, position), (blocks,), jnp.float32, low / len(split), largest / len(split)))
        factor_of = factor_of * jnp.repeat(steps, extent[position] // blocks).reshape([-1 if axis == position else 1 for axis in range(len(extent))])
    return factor_of


def centred(stream_key, shape, spread, bound, pieces=(), held_as=jnp.bfloat16):
    drawn = jax.random.normal(stream_key, shape, jnp.float32) * spread
    if len(pieces) > 0:
        drawn = level_of(stream_key, shape, pieces, -0.22, 0.18) * drawn
    return jnp.clip(drawn, min=-bound, max=bound).astype(held_as)


def setup_inputs(seed: int = 0, part: int = 0) -> dict:
    seeds = jax.random.split(jax.random.key(seed), 7)
    own_keys = jax.random.split(jax.random.fold_in(seeds[6], part), 7)
    return {
        "images": centred(own_keys[0], (VOLS, SLICES, 2, MATRIX, MATRIX), 1.0, 6.0, ((0, 2), (1, 4))),
        "coil_maps": centred(own_keys[1], (COILS, SLICES, 2, MATRIX, MATRIX), 0.5, 3.0, ((0, 2), (1, 4))),
        "kspace": centred(own_keys[2], (VOLS, GROUPS, COILS, 2, MATRIX, MATRIX), 2.0, 12.0, ((0, 2), (1, 4), (2, 2))),
        "shift_index": set_ends(jax.random.randint(seeds[3], (SLICES,), 0, MB), jax.random.fold_in(seeds[3], 1), 0, MB - 1).astype(jnp.int32),
        "phase_offset": jnp.clip(jax.random.uniform(seeds[4], (SLICES, MATRIX), jnp.float32, -3.140625, 3.140625), -3.140625, 3.140625),
        "group_order": jax.random.permutation(seeds[5], GROUPS).astype(jnp.int32),
    }


def to_half(values):
    return lax.optimization_barrier(values.astype(jnp.bfloat16)).astype(jnp.float32)

def fourier_tables(length):
    positions = jnp.arange(length, dtype=jnp.int32)
    product = positions[:, None] * positions[None, :] % length
    radians = 2.0 * math.pi / length * product.astype(jnp.float32)
    factor = 1.0 / math.sqrt(length)
    return ((jnp.cos(radians) * factor).astype(jnp.bfloat16), (-jnp.sin(radians) * factor).astype(jnp.bfloat16))

def slice_phases(shift_index, phase_offset, length):
    lines = (jnp.arange(length, dtype=jnp.int32) - length // 2).astype(jnp.float32)
    return 2.0 * math.pi / MB * (shift_index.astype(jnp.float32)[:, None] * lines[None, :]) + phase_offset

def reference(images, coil_maps, kspace, shift_index, phase_offset, group_order):
    hp = lax.Precision.HIGHEST
    cos_table, sin_table = fourier_tables(MATRIX)
    cos_full = cos_table.astype(jnp.float32)
    sin_full = sin_table.astype(jnp.float32)
    phase_angle = slice_phases(shift_index, phase_offset, MATRIX)
    cosine = jnp.cos(phase_angle)[None, :, :, None]
    sine = jnp.sin(phase_angle)[None, :, :, None]
    classes = jnp.arange(SLICES, dtype=jnp.int32) % GROUPS
    target = group_order[classes]
    onehot = (target[None, :] == jnp.arange(GROUPS, dtype=jnp.int32)[:, None]).astype(jnp.float32)
    image_re = images[:, :, 0].astype(jnp.float32)
    image_im = images[:, :, 1].astype(jnp.float32)

    def per_coil(packed):
        coil_map, measured = packed
        map_re = coil_map[:, 0].astype(jnp.float32)[None]
        map_im = coil_map[:, 1].astype(jnp.float32)[None]
        coil_re = to_half(map_re * image_re - map_im * image_im)
        coil_im = to_half(map_re * image_im + map_im * image_re)
        half_re = to_half(jnp.einsum('ky,vsyx->vskx', cos_full, coil_re, precision=hp) - jnp.einsum('ky,vsyx->vskx', sin_full, coil_im, precision=hp))
        half_im = to_half(jnp.einsum('ky,vsyx->vskx', cos_full, coil_im, precision=hp) + jnp.einsum('ky,vsyx->vskx', sin_full, coil_re, precision=hp))
        spec_re = jnp.einsum('vsyx,kx->vsyk', half_re, cos_full, precision=hp) - jnp.einsum('vsyx,kx->vsyk', half_im, sin_full, precision=hp)
        spec_im = jnp.einsum('vsyx,kx->vsyk', half_re, sin_full, precision=hp) + jnp.einsum('vsyx,kx->vsyk', half_im, cos_full, precision=hp)
        shift_re = to_half(spec_re * cosine - spec_im * sine)
        shift_im = to_half(spec_re * sine + spec_im * cosine)
        alias_re = jnp.einsum('gs,vsyx->vgyx', onehot, shift_re, precision=hp)
        alias_im = jnp.einsum('gs,vsyx->vgyx', onehot, shift_im, precision=hp)
        resid_re = to_half(alias_re - measured[:, :, 0].astype(jnp.float32))
        resid_im = to_half(alias_im - measured[:, :, 1].astype(jnp.float32))
        chosen_re = resid_re[:, target]
        chosen_im = resid_im[:, target]
        return lax.optimization_barrier(jnp.sum(chosen_im * shift_re - chosen_re * shift_im, axis=(0, 3)))
    per_coil_grad = lax.map(per_coil, (coil_maps, jnp.moveaxis(kspace, 2, 0)))
    return lax.optimization_barrier(jnp.sum(per_coil_grad, axis=0)) * (1.0 / (COILS * VOLS))
```

```python
import functools
import math

import jax
import jax.numpy as jnp
import numpy as np
from jax import lax
from jax.experimental import pallas as pl
from jax.experimental.pallas import tpu as pltpu
from jax.sharding import PartitionSpec as P

MB = 8


def fourier_tables(length):
    positions = jnp.arange(length, dtype=jnp.int32)
    product = positions[:, None] * positions[None, :] % length
    radians = 2.0 * math.pi / length * product.astype(jnp.float32)
    factor = 1.0 / math.sqrt(length)
    return (
        (jnp.cos(radians) * factor).astype(jnp.bfloat16),
        (-jnp.sin(radians) * factor).astype(jnp.bfloat16),
    )


def slice_phases(shift_index, phase_offset, length):
    lines = (jnp.arange(length, dtype=jnp.int32) - length // 2).astype(jnp.float32)
    return (
        2.0 * math.pi / MB * (shift_index.astype(jnp.float32)[:, None] * lines[None, :])
        + phase_offset
    )


ROWS = 32
MESH = pl.DeviceIdType.MESH
F32 = jnp.float32
BF16 = jnp.bfloat16


def round_up(value, unit):
    return -(-value // unit) * unit


def static_tables(length):
    positions = np.arange(length, dtype=np.int32)
    product = positions[:, None] * positions[None, :] % length
    radians = np.float32(2.0 * math.pi / length) * product.astype(np.float32)
    factor = np.float32(1.0 / math.sqrt(length))
    cosine = (np.cos(radians) * factor).astype(jnp.bfloat16)
    sine = (-np.sin(radians) * factor).astype(jnp.bfloat16)
    return np.asarray(cosine, np.float32), np.asarray(sine, np.float32)


def stage_tables(length, coils):
    cosine, sine = static_tables(length)
    rows, wide = round_up(length, ROWS), round_up(length, 128)
    first = np.zeros((3, rows, length), np.float32)
    first[0, :length], first[1, :length], first[2, :length] = cosine, sine, -sine
    forward = np.zeros((coils, 2, length, coils * 2 * length), np.float32)
    back = np.zeros((coils * 2 * length, coils * 2 * wide), np.float32)
    for coil in range(coils):
        low = coil * 2 * length
        mid, top = low + length, low + 2 * length
        forward[coil, 0, :, low:mid], forward[coil, 0, :, mid:top] = cosine, sine
        forward[coil, 1, :, low:mid], forward[coil, 1, :, mid:top] = -sine, cosine
        at = coil * 2 * wide
        back[low:mid, at : at + length], back[mid:top, at : at + length] = cosine, sine
        at = at + wide
        back[low:mid, at : at + length], back[mid:top, at : at + length] = -sine, cosine
    return first.astype(jnp.bfloat16), forward.astype(jnp.bfloat16), back.astype(jnp.bfloat16)


def kernel(
    sizes,
    order_ref,
    trig_ref,
    images_ref,
    maps_ref,
    measured_ref,
    first_ref,
    forward_ref,
    back_ref,
    out_ref,
    turned,
    own,
    to_right,
    to_left,
    from_left,
    from_right,
    columns,
    shares,
    right_send,
    left_send,
    left_recv,
    right_recv,
    share_send,
    share_recv,
):
    groups, coil_axis, vol_axis = sizes
    per_device = images_ref.shape[1]
    length = images_ref.shape[-1]
    coils = maps_ref.shape[0]
    rows, wide = first_ref.shape[1], turned.shape[-1] // (2 * coils)
    spread = per_device // groups
    parts = rows // ROWS
    total = groups * parts
    spot = lax.axis_index("slc")
    coil_at, vol_at = lax.axis_index("coil"), lax.axis_index("vol")
    has_left, has_right = spot > 0, spot < groups - 1
    peers = coil_axis * vol_axis
    mine = coil_at * vol_axis + vol_at

    def peer(distance):
        other = lax.rem(mine + distance, peers)
        return {"coil": other // vol_axis, "vol": lax.rem(other, vol_axis)}

    barrier = pltpu.get_barrier_semaphore()

    @pl.when(has_left)
    def _():
        pl.semaphore_signal(barrier, inc=1, device_id={"slc": spot - 1}, device_id_type=MESH)

    @pl.when(has_right)
    def _():
        pl.semaphore_signal(barrier, inc=1, device_id={"slc": spot + 1}, device_id_type=MESH)

    for distance in range(1, peers):
        pl.semaphore_signal(barrier, inc=1, device_id=peer(distance), device_id_type=MESH)

    def right_copy(chunk):
        return pltpu.make_async_remote_copy(
            src_ref=to_right.at[chunk],
            dst_ref=from_left.at[chunk],
            send_sem=right_send.at[chunk],
            recv_sem=left_recv.at[chunk],
            device_id={"slc": spot + 1},
            device_id_type=MESH,
        )

    def left_copy(chunk):
        return pltpu.make_async_remote_copy(
            src_ref=to_left.at[chunk],
            dst_ref=from_right.at[chunk],
            send_sem=left_send.at[chunk],
            recv_sem=right_recv.at[chunk],
            device_id={"slc": spot - 1},
            device_id_type=MESH,
        )

    turned[...] = jnp.zeros_like(turned)
    columns[...] = jnp.zeros_like(columns)

    def dot(left, right):
        return jnp.dot(left, right, preferred_element_type=F32)

    def compute(group):
        sums = [[None, None] for _ in range(coils)]
        for step in range(spread):
            within = group + step * groups
            image_re = images_ref[0, within, 0].astype(F32)
            image_im = images_ref[0, within, 1].astype(F32)
            cosine = trig_ref[:, 2 * within : 2 * within + 1]
            sine = trig_ref[:, 2 * within + 1 : 2 * within + 2]
            for coil in range(coils):
                map_re = maps_ref[coil, within, 0].astype(F32)
                map_im = maps_ref[coil, within, 1].astype(F32)
                coil_re = (map_re * image_re - map_im * image_im).astype(BF16)
                coil_im = (map_re * image_im + map_im * image_re).astype(BF16)
                part_re = dot(first_ref[0], coil_re) + dot(first_ref[2], coil_im)
                part_im = dot(first_ref[0], coil_im) + dot(first_ref[1], coil_re)
                turn_re = part_re * cosine - part_im * sine
                turn_im = part_re * sine + part_im * cosine
                at = coil * 2 * wide
                turned[within, :, at : at + length] = (-turn_im).astype(BF16)
                turned[within, :, at + wide : at + wide + length] = turn_re.astype(BF16)
                for which, value in enumerate((turn_re, turn_im)):
                    before = sums[coil][which]
                    sums[coil][which] = value if before is None else before + value
        spectrum = None
        for coil in range(coils):
            for which in range(2):
                term = dot(sums[coil][which].astype(BF16), forward_ref[coil, which])
                spectrum = term if spectrum is None else spectrum + term
        held = jnp.where(order_ref[group] == spot, F32(1.0), F32(0.0))
        spectrum = spectrum - held * measured_ref[...].astype(F32)
        own[group * parts : (group + 1) * parts] = spectrum.reshape(parts, ROWS, -1)

        @pl.when(jnp.logical_not(has_left))
        def _():
            for chunk in range(group * parts, (group + 1) * parts):
                to_right[chunk] = own[chunk].astype(BF16)
                right_copy(chunk).start()

        @pl.when(jnp.logical_not(has_right))
        def _():
            for chunk in range(group * parts, (group + 1) * parts):
                to_left[chunk] = own[chunk].astype(BF16)
                left_copy(chunk).start()

    late_right = jnp.maximum(0, 2 * spot - (groups - 1))
    late_left = jnp.maximum(0, (groups - 1) - 2 * spot)

    def wave(tick, carry):
        chunk = tick - late_right

        @pl.when(has_left & (chunk >= 0) & (chunk < total))
        def _():
            right_copy(chunk).wait_recv()

            @pl.when(has_right)
            def _():
                to_right[chunk] = (from_left[chunk].astype(F32) + own[chunk]).astype(BF16)
                right_copy(chunk).start()

        other = tick - late_left

        @pl.when(has_right & (other >= 0) & (other < total))
        def _():
            left_copy(other).wait_recv()

            @pl.when(has_left)
            def _():
                to_left[other] = (from_right[other].astype(F32) + own[other]).astype(BF16)
                left_copy(other).start()

        return carry

    def gradient(group):
        span = pl.ds(group * parts, parts)
        value = own[span]
        value = value + jnp.where(has_left, from_left[span].astype(F32), F32(0.0))
        value = value + jnp.where(has_right, from_right[span].astype(F32), F32(0.0))
        value = value.reshape(rows, -1).astype(BF16)
        pulled = dot(value, back_ref[...])
        for step in range(spread):
            within = group + step * groups
            product = pulled * turned[within].astype(F32)
            columns[0:rows, within : within + 1] = jnp.sum(product, axis=1, keepdims=True)

    def ticks(group):
        low = 0 if group == 0 else group * parts + groups - 1
        lax.fori_loop(low, (group + 1) * parts + groups - 1, wave, 0)

    arrivals = has_left.astype(jnp.int32) + has_right.astype(jnp.int32) + (peers - 1)
    pl.semaphore_wait(barrier, arrivals)
    compute(0)
    for group in range(1, groups):
        compute(group)
        if group < groups - 1:
            ticks(group - 1)
    for group in range(groups):
        if group >= max(groups - 2, 0):
            ticks(group)
        gradient(group)

    shares[mine] = columns[...].T[:per_device]

    def share_copy(distance):
        return pltpu.make_async_remote_copy(
            src_ref=shares.at[mine],
            dst_ref=shares.at[mine],
            send_sem=share_send.at[distance],
            recv_sem=share_recv.at[distance],
            device_id=peer(distance),
            device_id_type=MESH,
        )

    for distance in range(1, peers):
        share_copy(distance).start()

    @pl.when(has_right)
    def _():
        def done(chunk, carry):
            right_copy(chunk).wait_send()
            return carry

        lax.fori_loop(0, total, done, 0)

    @pl.when(has_left)
    def _():
        def done(chunk, carry):
            left_copy(chunk).wait_send()
            return carry

        lax.fori_loop(0, total, done, 0)

    for distance in range(1, peers):
        share_copy(distance).wait()
    result = shares[0]
    for other in range(1, peers):
        result = result + shares[other]
    out_ref[...] = result[:, :length] * (1.0 / (coils * peers))


def fused(images, coil_maps, kspace, shift_index, phase_offset, group_order):
    per_device, length = images.shape[1], images.shape[-1]
    coils = coil_maps.shape[0]
    groups = lax.axis_size("slc")
    sizes = (groups, lax.axis_size("coil"), lax.axis_size("vol"))
    peers = sizes[1] * sizes[2]
    first, forward, back = stage_tables(length, coils)
    rows, wide = first.shape[1], back.shape[1] // (2 * coils)
    width = coils * 2 * length
    angle = slice_phases(shift_index, phase_offset, length)
    trig = jnp.stack([jnp.cos(angle), jnp.sin(angle)], axis=1).reshape(2 * per_device, length)
    trig = jnp.pad(trig.T, ((0, rows - length), (0, 0)))
    measured = jnp.moveaxis(kspace[0, 0], 2, 0).reshape(length, width)
    measured = jnp.pad(measured, ((0, rows - length), (0, 0)))
    chunks = groups * rows // ROWS
    vmem = pl.BlockSpec(memory_space=pltpu.VMEM)
    smem = pl.BlockSpec(memory_space=pltpu.SMEM)
    block = pltpu.VMEM((chunks, ROWS, width), BF16)
    side = pltpu.SemaphoreType.DMA((chunks,))
    return pl.pallas_call(
        functools.partial(kernel, sizes),
        out_shape=jax.ShapeDtypeStruct((per_device, length), F32),
        in_specs=[smem] + [vmem] * 7,
        out_specs=vmem,
        scratch_shapes=[
            pltpu.VMEM((per_device, rows, coils * 2 * wide), BF16),
            pltpu.VMEM((chunks, ROWS, width), F32),
            block,
            block,
            block,
            block,
            pltpu.VMEM((wide, 128), F32),
            pltpu.VMEM((peers, per_device, wide), F32),
            side,
            side,
            side,
            side,
            pltpu.SemaphoreType.DMA((peers,)),
            pltpu.SemaphoreType.DMA((peers,)),
        ],
        compiler_params=pltpu.CompilerParams(
            collective_id=0, has_side_effects=True, vmem_limit_bytes=60 * 2**20
        ),
    )(
        group_order,
        trig,
        images,
        coil_maps,
        measured,
        jnp.asarray(first),
        jnp.asarray(forward),
        jnp.asarray(back),
    )


def program(images, coil_maps, kspace, shift_index, phase_offset, group_order):
    arguments = (images, coil_maps, kspace, shift_index, phase_offset, group_order)
    groups = lax.axis_size("slc")
    even = images.shape[1] % groups == 0 and images.shape[0] == 1 and kspace.shape[1] == 1
    if even and images.shape[1] <= 128 and groups > 2:
        return fused(*arguments)
    return body(*arguments)


def body(images, coil_maps, kspace, shift_index, phase_offset, group_order):
    per_device = images.shape[1]
    matrix = images.shape[-1]
    groups = lax.axis_size("slc")
    spread = max(1, per_device // groups)
    slot_count = groups * spread
    cos_table, sin_table = fourier_tables(matrix)
    section_one = jnp.stack([jnp.stack([cos_table, -sin_table]), jnp.stack([sin_table, cos_table])])
    section_two = jnp.stack([jnp.stack([cos_table, sin_table]), jnp.stack([-sin_table, cos_table])])
    image_re = images[:, None, :, 0].astype(jnp.float32)
    image_im = images[:, None, :, 1].astype(jnp.float32)
    map_re = coil_maps[None, :, :, 0].astype(jnp.float32)
    map_im = coil_maps[None, :, :, 1].astype(jnp.float32)
    coil_image = jnp.stack(
        [map_re * image_re - map_im * image_im, map_re * image_im + map_im * image_re], axis=3
    ).astype(jnp.bfloat16)
    partly = jnp.einsum(
        "pqky,tcsqyx->tcspkx", section_one, coil_image, preferred_element_type=jnp.float32
    ).astype(jnp.bfloat16)
    spectra = jnp.einsum(
        "tcsqyx,qpkx->tcspyk", partly, section_two, preferred_element_type=jnp.float32
    )
    phase_angle = slice_phases(shift_index, phase_offset, matrix)
    cosine = jnp.cos(phase_angle)[None, None, :, :, None]
    sine = jnp.sin(phase_angle)[None, None, :, :, None]
    spec_re = spectra[:, :, :, 0]
    spec_im = spectra[:, :, :, 1]
    shifted = jnp.stack(
        [spec_re * cosine - spec_im * sine, spec_re * sine + spec_im * cosine], axis=3
    ).astype(jnp.bfloat16)
    position = lax.axis_index("slc")
    within = jnp.arange(per_device, dtype=jnp.int32)
    classes = (position * per_device + within) % groups
    class_match = (classes[:, None] == jnp.arange(groups, dtype=jnp.int32)[None, :]).astype(
        jnp.int32
    )
    target = jnp.sum(class_match * group_order[None, :], axis=1)
    slot_index = target * spread + within // groups
    onehot = (jnp.arange(slot_count, dtype=jnp.int32)[:, None] == slot_index[None, :]).astype(
        jnp.int32
    )
    source = jnp.sum(onehot * within[None, :], axis=1)
    filled = jnp.sum(onehot, axis=1)
    outgoing = jnp.take(shifted, source, axis=2)
    outgoing = jnp.where(
        filled[None, None, :, None, None, None] > 0, outgoing, jnp.zeros_like(outgoing)
    )
    incoming = lax.all_to_all(outgoing, "slc", split_axis=2, concat_axis=2, tiled=True)
    aliased = jnp.sum(incoming, axis=2, dtype=jnp.float32)
    residual = (aliased - kspace[:, 0].astype(jnp.float32)).astype(jnp.bfloat16)
    partial_value = jnp.einsum(
        "tcpyx,tcyx->py",
        incoming[:, :, :, 0],
        residual[:, :, 1],
        preferred_element_type=jnp.float32,
    )
    partial_value = partial_value - jnp.einsum(
        "tcpyx,tcyx->py",
        incoming[:, :, :, 1],
        residual[:, :, 0],
        preferred_element_type=jnp.float32,
    )
    returned = lax.all_to_all(partial_value, "slc", split_axis=0, concat_axis=0, tiled=True)
    local_grad = jnp.dot(onehot.T.astype(jnp.float32), returned, precision=lax.Precision.HIGHEST)
    summed = lax.psum(local_grad, "coil")
    summed = lax.psum(summed, "vol")
    factor = 1.0 / (
        coil_maps.shape[0] * lax.axis_size("coil") * images.shape[0] * lax.axis_size("vol")
    )
    return summed * factor


def solution(mesh):
    placed = (
        P(("grp", "vol"), "slc", None, None, None),
        P(("grp", "coil"), "slc", None, None, None),
        P(("grp", "vol"), "slc", "coil", None, None, None),
        P("slc"),
        P("slc", None),
        P(),
    )
    return jax.shard_map(
        program, mesh=mesh, in_specs=placed, out_specs=P(("grp", "slc"), None), check_vma=False
    )
```

```python
import functools
import math

import jax
import jax.numpy as jnp
import numpy as np
from jax import lax
from jax.experimental import pallas as pl
from jax.experimental.pallas import tpu as pltpu
from jax.sharding import PartitionSpec as P

MB = 8


def fourier_tables(length):
    positions = jnp.arange(length, dtype=jnp.int32)
    product = positions[:, None] * positions[None, :] % length
    radians = 2.0 * math.pi / length * product.astype(jnp.float32)
    factor = 1.0 / math.sqrt(length)
    return (
        (jnp.cos(radians) * factor).astype(jnp.bfloat16),
        (-jnp.sin(radians) * factor).astype(jnp.bfloat16),
    )


def slice_phases(shift_index, phase_offset, length):
    lines = (jnp.arange(length, dtype=jnp.int32) - length // 2).astype(jnp.float32)
    return (
        2.0 * math.pi / MB * (shift_index.astype(jnp.float32)[:, None] * lines[None, :])
        + phase_offset
    )


ROWS = 32
LAG = 3
MESH = pl.DeviceIdType.MESH
F32 = jnp.float32
BF16 = jnp.bfloat16


def round_up(value, unit):
    return -(-value // unit) * unit


def static_tables(length):
    positions = np.arange(length, dtype=np.int32)
    product = positions[:, None] * positions[None, :] % length
    radians = np.float32(2.0 * math.pi / length) * product.astype(np.float32)
    factor = np.float32(1.0 / math.sqrt(length))
    cosine = (np.cos(radians) * factor).astype(jnp.bfloat16)
    sine = (-np.sin(radians) * factor).astype(jnp.bfloat16)
    return np.asarray(cosine, np.float32), np.asarray(sine, np.float32)


def stage_tables(length, coils):
    cosine, sine = static_tables(length)
    rows, wide = round_up(length, ROWS), round_up(length, 128)
    first = np.zeros((3, rows, length), np.float32)
    first[0, :length], first[1, :length], first[2, :length] = cosine, sine, -sine
    forward = np.zeros((coils, 2, length, coils * 2 * length), np.float32)
    back = np.zeros((coils * 2 * length, coils * 2 * wide), np.float32)
    for coil in range(coils):
        low = coil * 2 * length
        mid, top = low + length, low + 2 * length
        forward[coil, 0, :, low:mid], forward[coil, 0, :, mid:top] = cosine, sine
        forward[coil, 1, :, low:mid], forward[coil, 1, :, mid:top] = -sine, cosine
        at = coil * 2 * wide
        back[low:mid, at : at + length], back[mid:top, at : at + length] = cosine, sine
        at = at + wide
        back[low:mid, at : at + length], back[mid:top, at : at + length] = -sine, cosine
    return first.astype(jnp.bfloat16), forward.astype(jnp.bfloat16), back.astype(jnp.bfloat16)


def kernel(
    sizes,
    order_ref,
    trig_ref,
    images_ref,
    maps_ref,
    measured_ref,
    first_ref,
    forward_ref,
    back_ref,
    out_ref,
    turned,
    own,
    to_right,
    to_left,
    from_left,
    from_right,
    columns,
    shares,
    right_send,
    left_send,
    left_recv,
    right_recv,
    share_send,
    share_recv,
):
    groups, coil_axis, vol_axis = sizes
    per_device = images_ref.shape[1]
    length = images_ref.shape[-1]
    coils = maps_ref.shape[0]
    rows, wide = first_ref.shape[1], turned.shape[-1] // (2 * coils)
    spread = per_device // groups
    parts = rows // ROWS
    total = groups * parts
    spot = lax.axis_index("slc")
    coil_at, vol_at = lax.axis_index("coil"), lax.axis_index("vol")
    has_left, has_right = spot > 0, spot < groups - 1
    peers = coil_axis * vol_axis
    mine = coil_at * vol_axis + vol_at

    def peer(distance):
        other = lax.rem(mine + distance, peers)
        return {"coil": other // vol_axis, "vol": lax.rem(other, vol_axis)}

    barrier = pltpu.get_barrier_semaphore()

    @pl.when(has_left)
    def _():
        pl.semaphore_signal(barrier, inc=1, device_id={"slc": spot - 1}, device_id_type=MESH)

    @pl.when(has_right)
    def _():
        pl.semaphore_signal(barrier, inc=1, device_id={"slc": spot + 1}, device_id_type=MESH)

    for distance in range(1, peers):
        pl.semaphore_signal(barrier, inc=1, device_id=peer(distance), device_id_type=MESH)

    def right_copy(chunk):
        return pltpu.make_async_remote_copy(
            src_ref=to_right.at[chunk],
            dst_ref=from_left.at[chunk],
            send_sem=right_send.at[chunk],
            recv_sem=left_recv.at[chunk],
            device_id={"slc": spot + 1},
            device_id_type=MESH,
        )

    def left_copy(chunk):
        return pltpu.make_async_remote_copy(
            src_ref=to_left.at[chunk],
            dst_ref=from_right.at[chunk],
            send_sem=left_send.at[chunk],
            recv_sem=right_recv.at[chunk],
            device_id={"slc": spot - 1},
            device_id_type=MESH,
        )

    turned[...] = jnp.zeros_like(turned)
    columns[...] = jnp.zeros_like(columns)

    def dot(left, right):
        return jnp.dot(left, right, preferred_element_type=F32)

    def compute(group):
        sums = [[None, None] for _ in range(coils)]
        for step in range(spread):
            within = group + step * groups
            image_re = images_ref[0, within, 0].astype(F32)
            image_im = images_ref[0, within, 1].astype(F32)
            cosine = trig_ref[:, 2 * within : 2 * within + 1]
            sine = trig_ref[:, 2 * within + 1 : 2 * within + 2]
            for coil in range(coils):
                map_re = maps_ref[coil, within, 0].astype(F32)
                map_im = maps_ref[coil, within, 1].astype(F32)
                coil_re = (map_re * image_re - map_im * image_im).astype(BF16)
                coil_im = (map_re * image_im + map_im * image_re).astype(BF16)
                part_re = dot(first_ref[0], coil_re) + dot(first_ref[2], coil_im)
                part_im = dot(first_ref[0], coil_im) + dot(first_ref[1], coil_re)
                turn_re = part_re * cosine - part_im * sine
                turn_im = part_re * sine + part_im * cosine
                at = coil * 2 * wide
                turned[within, :, at : at + length] = (-turn_im).astype(BF16)
                turned[within, :, at + wide : at + wide + length] = turn_re.astype(BF16)
                for which, value in enumerate((turn_re, turn_im)):
                    before = sums[coil][which]
                    sums[coil][which] = value if before is None else before + value
        spectrum = None
        for coil in range(coils):
            for which in range(2):
                term = dot(sums[coil][which].astype(BF16), forward_ref[coil, which])
                spectrum = term if spectrum is None else spectrum + term
        held = jnp.where(order_ref[group] == spot, F32(1.0), F32(0.0))
        spectrum = spectrum - held * measured_ref[...].astype(F32)
        own[group * parts : (group + 1) * parts] = spectrum.reshape(parts, ROWS, -1)

        @pl.when(jnp.logical_not(has_left))
        def _():
            for chunk in range(group * parts, (group + 1) * parts):
                to_right[chunk] = own[chunk].astype(BF16)
                right_copy(chunk).start()

        @pl.when(jnp.logical_not(has_right))
        def _():
            for chunk in range(group * parts, (group + 1) * parts):
                to_left[chunk] = own[chunk].astype(BF16)
                left_copy(chunk).start()

    between = jnp.where(has_left & has_right, LAG, 0)
    late_right = between * jnp.maximum(0, 2 * spot - (groups - 1))
    late_left = between * jnp.maximum(0, (groups - 1) - 2 * spot)
    extra = LAG * (groups - 3)

    def wave(tick, carry):
        chunk = tick - late_right

        @pl.when(has_left & (chunk >= 0) & (chunk < total))
        def _():
            right_copy(chunk).wait_recv()

            @pl.when(has_right)
            def _():
                to_right[chunk] = (from_left[chunk].astype(F32) + own[chunk]).astype(BF16)
                right_copy(chunk).start()

        other = tick - late_left

        @pl.when(has_right & (other >= 0) & (other < total))
        def _():
            left_copy(other).wait_recv()

            @pl.when(has_left)
            def _():
                to_left[other] = (from_right[other].astype(F32) + own[other]).astype(BF16)
                left_copy(other).start()

        return carry

    def gradient(group):
        span = pl.ds(group * parts, parts)
        value = own[span]
        value = value + jnp.where(has_left, from_left[span].astype(F32), F32(0.0))
        value = value + jnp.where(has_right, from_right[span].astype(F32), F32(0.0))
        value = value.reshape(rows, -1).astype(BF16)
        pulled = dot(value, back_ref[...])
        for step in range(spread):
            within = group + step * groups
            product = pulled * turned[within].astype(F32)
            columns[0:rows, within : within + 1] = jnp.sum(product, axis=1, keepdims=True)

    def ticks(group):
        low = 0 if group == 0 else group * parts + extra
        high = (group + 1) * parts + extra
        end_low = group * parts if group == groups - 1 else 0
        end_high = (group + 1) * parts if group >= groups - 2 else 0
        inner = has_left & has_right
        lax.fori_loop(
            jnp.where(inner, low, end_low), jnp.where(inner, high, end_high), wave, 0
        )

    arrivals = has_left.astype(jnp.int32) + has_right.astype(jnp.int32) + (peers - 1)
    pl.semaphore_wait(barrier, arrivals)
    compute(0)
    for group in range(1, groups):
        compute(group)
        if group < groups - 1:
            ticks(group - 1)
    ticks(groups - 2)
    for group in range(groups - 2):
        gradient(group)
    ticks(groups - 1)
    for group in range(groups - 2, groups):
        gradient(group)

    shares[mine] = columns[...].T[:per_device]

    def share_copy(distance):
        return pltpu.make_async_remote_copy(
            src_ref=shares.at[mine],
            dst_ref=shares.at[mine],
            send_sem=share_send.at[distance],
            recv_sem=share_recv.at[distance],
            device_id=peer(distance),
            device_id_type=MESH,
        )

    for distance in range(1, peers):
        share_copy(distance).start()

    @pl.when(has_right)
    def _():
        def done(chunk, carry):
            right_copy(chunk).wait_send()
            return carry

        lax.fori_loop(0, total, done, 0)

    @pl.when(has_left)
    def _():
        def done(chunk, carry):
            left_copy(chunk).wait_send()
            return carry

        lax.fori_loop(0, total, done, 0)

    for distance in range(1, peers):
        share_copy(distance).wait()
    result = shares[0]
    for other in range(1, peers):
        result = result + shares[other]
    out_ref[...] = result[:, :length] * (1.0 / (coils * peers))


def fused(images, coil_maps, kspace, shift_index, phase_offset, group_order):
    per_device, length = images.shape[1], images.shape[-1]
    coils = coil_maps.shape[0]
    groups = lax.axis_size("slc")
    sizes = (groups, lax.axis_size("coil"), lax.axis_size("vol"))
    peers = sizes[1] * sizes[2]
    first, forward, back = stage_tables(length, coils)
    rows, wide = first.shape[1], back.shape[1] // (2 * coils)
    width = coils * 2 * length
    angle = slice_phases(shift_index, phase_offset, length)
    trig = jnp.stack([jnp.cos(angle), jnp.sin(angle)], axis=1).reshape(2 * per_device, length)
    trig = jnp.pad(trig.T, ((0, rows - length), (0, 0)))
    measured = jnp.moveaxis(kspace[0, 0], 2, 0).reshape(length, width)
    measured = jnp.pad(measured, ((0, rows - length), (0, 0)))
    chunks = groups * rows // ROWS
    vmem = pl.BlockSpec(memory_space=pltpu.VMEM)
    smem = pl.BlockSpec(memory_space=pltpu.SMEM)
    block = pltpu.VMEM((chunks, ROWS, width), BF16)
    side = pltpu.SemaphoreType.DMA((chunks,))
    return pl.pallas_call(
        functools.partial(kernel, sizes),
        out_shape=jax.ShapeDtypeStruct((per_device, length), F32),
        in_specs=[smem] + [vmem] * 7,
        out_specs=vmem,
        scratch_shapes=[
            pltpu.VMEM((per_device, rows, coils * 2 * wide), BF16),
            pltpu.VMEM((chunks, ROWS, width), F32),
            block,
            block,
            block,
            block,
            pltpu.VMEM((wide, 128), F32),
            pltpu.VMEM((peers, per_device, wide), F32),
            side,
            side,
            side,
            side,
            pltpu.SemaphoreType.DMA((peers,)),
            pltpu.SemaphoreType.DMA((peers,)),
        ],
        compiler_params=pltpu.CompilerParams(
            collective_id=0, has_side_effects=True, vmem_limit_bytes=60 * 2**20
        ),
    )(
        group_order,
        trig,
        images,
        coil_maps,
        measured,
        jnp.asarray(first),
        jnp.asarray(forward),
        jnp.asarray(back),
    )


def program(images, coil_maps, kspace, shift_index, phase_offset, group_order):
    arguments = (images, coil_maps, kspace, shift_index, phase_offset, group_order)
    groups = lax.axis_size("slc")
    even = images.shape[1] % groups == 0 and images.shape[0] == 1 and kspace.shape[1] == 1
    if even and images.shape[1] <= 128 and groups > 2:
        return fused(*arguments)
    return body(*arguments)


def body(images, coil_maps, kspace, shift_index, phase_offset, group_order):
    per_device = images.shape[1]
    matrix = images.shape[-1]
    groups = lax.axis_size("slc")
    spread = max(1, per_device // groups)
    slot_count = groups * spread
    cos_table, sin_table = fourier_tables(matrix)
    section_one = jnp.stack([jnp.stack([cos_table, -sin_table]), jnp.stack([sin_table, cos_table])])
    section_two = jnp.stack([jnp.stack([cos_table, sin_table]), jnp.stack([-sin_table, cos_table])])
    image_re = images[:, None, :, 0].astype(jnp.float32)
    image_im = images[:, None, :, 1].astype(jnp.float32)
    map_re = coil_maps[None, :, :, 0].astype(jnp.float32)
    map_im = coil_maps[None, :, :, 1].astype(jnp.float32)
    coil_image = jnp.stack(
        [map_re * image_re - map_im * image_im, map_re * image_im + map_im * image_re], axis=3
    ).astype(jnp.bfloat16)
    partly = jnp.einsum(
        "pqky,tcsqyx->tcspkx", section_one, coil_image, preferred_element_type=jnp.float32
    ).astype(jnp.bfloat16)
    spectra = jnp.einsum(
        "tcsqyx,qpkx->tcspyk", partly, section_two, preferred_element_type=jnp.float32
    )
    phase_angle = slice_phases(shift_index, phase_offset, matrix)
    cosine = jnp.cos(phase_angle)[None, None, :, :, None]
    sine = jnp.sin(phase_angle)[None, None, :, :, None]
    spec_re = spectra[:, :, :, 0]
    spec_im = spectra[:, :, :, 1]
    shifted = jnp.stack(
        [spec_re * cosine - spec_im * sine, spec_re * sine + spec_im * cosine], axis=3
    ).astype(jnp.bfloat16)
    position = lax.axis_index("slc")
    within = jnp.arange(per_device, dtype=jnp.int32)
    classes = (position * per_device + within) % groups
    class_match = (classes[:, None] == jnp.arange(groups, dtype=jnp.int32)[None, :]).astype(
        jnp.int32
    )
    target = jnp.sum(class_match * group_order[None, :], axis=1)
    slot_index = target * spread + within // groups
    onehot = (jnp.arange(slot_count, dtype=jnp.int32)[:, None] == slot_index[None, :]).astype(
        jnp.int32
    )
    source = jnp.sum(onehot * within[None, :], axis=1)
    filled = jnp.sum(onehot, axis=1)
    outgoing = jnp.take(shifted, source, axis=2)
    outgoing = jnp.where(
        filled[None, None, :, None, None, None] > 0, outgoing, jnp.zeros_like(outgoing)
    )
    incoming = lax.all_to_all(outgoing, "slc", split_axis=2, concat_axis=2, tiled=True)
    aliased = jnp.sum(incoming, axis=2, dtype=jnp.float32)
    residual = (aliased - kspace[:, 0].astype(jnp.float32)).astype(jnp.bfloat16)
    partial_value = jnp.einsum(
        "tcpyx,tcyx->py",
        incoming[:, :, :, 0],
        residual[:, :, 1],
        preferred_element_type=jnp.float32,
    )
    partial_value = partial_value - jnp.einsum(
        "tcpyx,tcyx->py",
        incoming[:, :, :, 1],
        residual[:, :, 0],
        preferred_element_type=jnp.float32,
    )
    returned = lax.all_to_all(partial_value, "slc", split_axis=0, concat_axis=0, tiled=True)
    local_grad = jnp.dot(onehot.T.astype(jnp.float32), returned, precision=lax.Precision.HIGHEST)
    summed = lax.psum(local_grad, "coil")
    summed = lax.psum(summed, "vol")
    factor = 1.0 / (
        coil_maps.shape[0] * lax.axis_size("coil") * images.shape[0] * lax.axis_size("vol")
    )
    return summed * factor


def solution(mesh):
    placed = (
        P(("grp", "vol"), "slc", None, None, None),
        P(("grp", "coil"), "slc", None, None, None),
        P(("grp", "vol"), "slc", "coil", None, None, None),
        P("slc"),
        P("slc", None),
        P(),
    )
    return jax.shard_map(
        program, mesh=mesh, in_specs=placed, out_specs=P(("grp", "slc"), None), check_vma=False
    )
```

```python
import functools
import math

import jax
import jax.numpy as jnp
import numpy as np
from jax import lax
from jax.experimental import pallas as pl
from jax.experimental.pallas import tpu as pltpu
from jax.sharding import PartitionSpec as P

MB = 8


def fourier_tables(length):
    positions = jnp.arange(length, dtype=jnp.int32)
    product = positions[:, None] * positions[None, :] % length
    radians = 2.0 * math.pi / length * product.astype(jnp.float32)
    factor = 1.0 / math.sqrt(length)
    return (
        (jnp.cos(radians) * factor).astype(jnp.bfloat16),
        (-jnp.sin(radians) * factor).astype(jnp.bfloat16),
    )


def slice_phases(shift_index, phase_offset, length):
    lines = (jnp.arange(length, dtype=jnp.int32) - length // 2).astype(jnp.float32)
    return (
        2.0 * math.pi / MB * (shift_index.astype(jnp.float32)[:, None] * lines[None, :])
        + phase_offset
    )


ROWS = 32
LAG = 3
MESH = pl.DeviceIdType.MESH
F32 = jnp.float32
BF16 = jnp.bfloat16


def round_up(value, unit):
    return -(-value // unit) * unit


def static_tables(length):
    positions = np.arange(length, dtype=np.int32)
    product = positions[:, None] * positions[None, :] % length
    radians = np.float32(2.0 * math.pi / length) * product.astype(np.float32)
    factor = np.float32(1.0 / math.sqrt(length))
    cosine = (np.cos(radians) * factor).astype(jnp.bfloat16)
    sine = (-np.sin(radians) * factor).astype(jnp.bfloat16)
    return np.asarray(cosine, np.float32), np.asarray(sine, np.float32)


def stage_tables(length, coils):
    cosine, sine = static_tables(length)
    rows, wide = round_up(length, ROWS), round_up(length, 128)
    first = np.zeros((3, rows, length), np.float32)
    first[0, :length], first[1, :length], first[2, :length] = cosine, sine, -sine
    forward = np.zeros((coils, 2, length, coils * 2 * length), np.float32)
    back = np.zeros((coils * 2 * length, coils * 2 * wide), np.float32)
    for coil in range(coils):
        low = coil * 2 * length
        mid, top = low + length, low + 2 * length
        forward[coil, 0, :, low:mid], forward[coil, 0, :, mid:top] = cosine, sine
        forward[coil, 1, :, low:mid], forward[coil, 1, :, mid:top] = -sine, cosine
        at = coil * 2 * wide
        back[low:mid, at : at + length], back[mid:top, at : at + length] = cosine, sine
        at = at + wide
        back[low:mid, at : at + length], back[mid:top, at : at + length] = -sine, cosine
    return first.astype(jnp.bfloat16), forward.astype(jnp.bfloat16), back.astype(jnp.bfloat16)


def kernel(
    sizes,
    order_ref,
    trig_in,
    images_ref,
    maps_ref,
    measured_in,
    first_ref,
    forward_ref,
    back_ref,
    out_ref,
    turned,
    own,
    to_right,
    to_left,
    from_left,
    from_right,
    columns,
    trig_ref,
    measured_ref,
    shares,
    right_send,
    left_send,
    left_recv,
    right_recv,
    share_send,
    share_recv,
):
    groups, coil_axis, vol_axis = sizes
    per_device = images_ref.shape[1]
    length = images_ref.shape[-1]
    coils = maps_ref.shape[0]
    rows, wide = first_ref.shape[1], turned.shape[-1] // (2 * coils)
    spread = per_device // groups
    parts = rows // ROWS
    total = groups * parts
    spot = lax.axis_index("slc")
    coil_at, vol_at = lax.axis_index("coil"), lax.axis_index("vol")
    has_left, has_right = spot > 0, spot < groups - 1
    peers = coil_axis * vol_axis
    mine = coil_at * vol_axis + vol_at

    def peer(distance):
        other = lax.rem(mine + distance, peers)
        return {"coil": other // vol_axis, "vol": lax.rem(other, vol_axis)}

    barrier = pltpu.get_barrier_semaphore()

    @pl.when(has_left)
    def _():
        pl.semaphore_signal(barrier, inc=1, device_id={"slc": spot - 1}, device_id_type=MESH)

    @pl.when(has_right)
    def _():
        pl.semaphore_signal(barrier, inc=1, device_id={"slc": spot + 1}, device_id_type=MESH)

    for distance in range(1, peers):
        pl.semaphore_signal(barrier, inc=1, device_id=peer(distance), device_id_type=MESH)

    def right_copy(chunk):
        return pltpu.make_async_remote_copy(
            src_ref=to_right.at[chunk],
            dst_ref=from_left.at[chunk],
            send_sem=right_send.at[chunk],
            recv_sem=left_recv.at[chunk],
            device_id={"slc": spot + 1},
            device_id_type=MESH,
        )

    def left_copy(chunk):
        return pltpu.make_async_remote_copy(
            src_ref=to_left.at[chunk],
            dst_ref=from_right.at[chunk],
            send_sem=left_send.at[chunk],
            recv_sem=right_recv.at[chunk],
            device_id={"slc": spot - 1},
            device_id_type=MESH,
        )

    turned[...] = jnp.zeros_like(turned)
    columns[...] = jnp.zeros_like(columns)
    trig_ref[...] = jnp.zeros_like(trig_ref)
    measured_ref[...] = jnp.zeros_like(measured_ref)
    trig_ref[:length] = trig_in[...]
    measured_ref[:length] = measured_in[...]

    def dot(left, right):
        return jnp.dot(left, right, preferred_element_type=F32)

    def compute(group):
        sums = [[None, None] for _ in range(coils)]
        for step in range(spread):
            within = group + step * groups
            image_re = images_ref[0, within, 0].astype(F32)
            image_im = images_ref[0, within, 1].astype(F32)
            cosine = trig_ref[:, within : within + 1]
            sine = trig_ref[:, per_device + within : per_device + within + 1]
            for coil in range(coils):
                coil_map = jnp.swapaxes(maps_ref[coil, within].astype(F32), 0, 1)
                map_re, map_im = coil_map[0], coil_map[1]
                coil_re = (map_re * image_re - map_im * image_im).astype(BF16)
                coil_im = (map_re * image_im + map_im * image_re).astype(BF16)
                part_re = dot(first_ref[0], coil_re) + dot(first_ref[2], coil_im)
                part_im = dot(first_ref[0], coil_im) + dot(first_ref[1], coil_re)
                turn_re = part_re * cosine - part_im * sine
                turn_im = part_re * sine + part_im * cosine
                at = coil * 2 * wide
                turned[within, :, at : at + length] = (-turn_im).astype(BF16)
                turned[within, :, at + wide : at + wide + length] = turn_re.astype(BF16)
                for which, value in enumerate((turn_re, turn_im)):
                    before = sums[coil][which]
                    sums[coil][which] = value if before is None else before + value
        spectrum = None
        for coil in range(coils):
            for which in range(2):
                term = dot(sums[coil][which].astype(BF16), forward_ref[coil, which])
                spectrum = term if spectrum is None else spectrum + term
        held = jnp.where(order_ref[group] == spot, F32(1.0), F32(0.0))
        spectrum = spectrum - held * measured_ref[...].astype(F32)
        own[group * parts : (group + 1) * parts] = spectrum.reshape(parts, ROWS, -1)

        @pl.when(jnp.logical_not(has_left))
        def _():
            for chunk in range(group * parts, (group + 1) * parts):
                to_right[chunk] = own[chunk].astype(BF16)
                right_copy(chunk).start()

        @pl.when(jnp.logical_not(has_right))
        def _():
            for chunk in range(group * parts, (group + 1) * parts):
                to_left[chunk] = own[chunk].astype(BF16)
                left_copy(chunk).start()

    between = jnp.where(has_left & has_right, LAG, 0)
    late_right = between * jnp.maximum(0, 2 * spot - (groups - 1))
    late_left = between * jnp.maximum(0, (groups - 1) - 2 * spot)
    extra = LAG * (groups - 3)

    def wave(tick, carry):
        chunk = tick - late_right

        @pl.when(has_left & (chunk >= 0) & (chunk < total))
        def _():
            right_copy(chunk).wait_recv()

            @pl.when(has_right)
            def _():
                to_right[chunk] = (from_left[chunk].astype(F32) + own[chunk]).astype(BF16)
                right_copy(chunk).start()

        other = tick - late_left

        @pl.when(has_right & (other >= 0) & (other < total))
        def _():
            left_copy(other).wait_recv()

            @pl.when(has_left)
            def _():
                to_left[other] = (from_right[other].astype(F32) + own[other]).astype(BF16)
                left_copy(other).start()

        return carry

    def gradient(group):
        span = pl.ds(group * parts, parts)
        value = own[span]
        value = value + jnp.where(has_left, from_left[span].astype(F32), F32(0.0))
        value = value + jnp.where(has_right, from_right[span].astype(F32), F32(0.0))
        value = value.reshape(rows, -1).astype(BF16)
        pulled = dot(value, back_ref[...])
        for step in range(spread):
            within = group + step * groups
            product = pulled * turned[within].astype(F32)
            columns[0:rows, within : within + 1] = jnp.sum(product, axis=1, keepdims=True)

    def ticks(group):
        low = 0 if group == 0 else group * parts + extra
        high = (group + 1) * parts + extra
        end_low = group * parts if group == groups - 1 else 0
        end_high = (group + 1) * parts if group >= groups - 2 else 0
        inner = has_left & has_right
        lax.fori_loop(
            jnp.where(inner, low, end_low), jnp.where(inner, high, end_high), wave, 0
        )

    arrivals = has_left.astype(jnp.int32) + has_right.astype(jnp.int32) + (peers - 1)
    pl.semaphore_wait(barrier, arrivals)
    compute(0)
    for group in range(1, groups):
        compute(group)
        if group < groups - 1:
            ticks(group - 1)
    ticks(groups - 2)
    for group in range(groups - 2):
        gradient(group)
    ticks(groups - 1)
    for group in range(groups - 2, groups):
        gradient(group)

    shares[mine] = columns[...].T[:per_device]

    def share_copy(distance):
        return pltpu.make_async_remote_copy(
            src_ref=shares.at[mine],
            dst_ref=shares.at[mine],
            send_sem=share_send.at[distance],
            recv_sem=share_recv.at[distance],
            device_id=peer(distance),
            device_id_type=MESH,
        )

    for distance in range(1, peers):
        share_copy(distance).start()

    @pl.when(has_right)
    def _():
        def done(chunk, carry):
            right_copy(chunk).wait_send()
            return carry

        lax.fori_loop(0, total, done, 0)

    @pl.when(has_left)
    def _():
        def done(chunk, carry):
            left_copy(chunk).wait_send()
            return carry

        lax.fori_loop(0, total, done, 0)

    for distance in range(1, peers):
        share_copy(distance).wait()
    result = shares[0]
    for other in range(1, peers):
        result = result + shares[other]
    out_ref[...] = result[:, :length] * (1.0 / (coils * peers))


def fused(images, coil_maps, kspace, shift_index, phase_offset, group_order):
    per_device, length = images.shape[1], images.shape[-1]
    coils = coil_maps.shape[0]
    groups = lax.axis_size("slc")
    sizes = (groups, lax.axis_size("coil"), lax.axis_size("vol"))
    peers = sizes[1] * sizes[2]
    first, forward, back = stage_tables(length, coils)
    rows, wide = first.shape[1], back.shape[1] // (2 * coils)
    width = coils * 2 * length
    angle = slice_phases(shift_index, phase_offset, length)
    trig = jnp.concatenate([jnp.cos(angle), jnp.sin(angle)], axis=0)
    trig = trig.T
    measured = jnp.moveaxis(kspace[0, 0], 2, 0).reshape(length, width)
    chunks = groups * rows // ROWS
    vmem = pl.BlockSpec(memory_space=pltpu.VMEM)
    smem = pl.BlockSpec(memory_space=pltpu.SMEM)
    block = pltpu.VMEM((chunks, ROWS, width), BF16)
    side = pltpu.SemaphoreType.DMA((chunks,))
    return pl.pallas_call(
        functools.partial(kernel, sizes),
        out_shape=jax.ShapeDtypeStruct((per_device, length), F32),
        in_specs=[smem] + [vmem] * 7,
        out_specs=vmem,
        scratch_shapes=[
            pltpu.VMEM((per_device, rows, coils * 2 * wide), BF16),
            pltpu.VMEM((chunks, ROWS, width), F32),
            block,
            block,
            block,
            block,
            pltpu.VMEM((wide, 128), F32),
            pltpu.VMEM((rows, 2 * per_device), F32),
            pltpu.VMEM((rows, width), BF16),
            pltpu.VMEM((peers, per_device, wide), F32),
            side,
            side,
            side,
            side,
            pltpu.SemaphoreType.DMA((peers,)),
            pltpu.SemaphoreType.DMA((peers,)),
        ],
        compiler_params=pltpu.CompilerParams(
            collective_id=0, has_side_effects=True, vmem_limit_bytes=60 * 2**20
        ),
    )(
        group_order,
        trig,
        images,
        jnp.swapaxes(coil_maps, 2, 3),
        measured,
        jnp.asarray(first),
        jnp.asarray(forward),
        jnp.asarray(back),
    )


def program(images, coil_maps, kspace, shift_index, phase_offset, group_order):
    arguments = (images, coil_maps, kspace, shift_index, phase_offset, group_order)
    groups = lax.axis_size("slc")
    even = images.shape[1] % groups == 0 and images.shape[0] == 1 and kspace.shape[1] == 1
    if even and images.shape[1] <= 128 and groups > 2:
        return fused(*arguments)
    return body(*arguments)


def body(images, coil_maps, kspace, shift_index, phase_offset, group_order):
    per_device = images.shape[1]
    matrix = images.shape[-1]
    groups = lax.axis_size("slc")
    spread = max(1, per_device // groups)
    slot_count = groups * spread
    cos_table, sin_table = fourier_tables(matrix)
    section_one = jnp.stack([jnp.stack([cos_table, -sin_table]), jnp.stack([sin_table, cos_table])])
    section_two = jnp.stack([jnp.stack([cos_table, sin_table]), jnp.stack([-sin_table, cos_table])])
    image_re = images[:, None, :, 0].astype(jnp.float32)
    image_im = images[:, None, :, 1].astype(jnp.float32)
    map_re = coil_maps[None, :, :, 0].astype(jnp.float32)
    map_im = coil_maps[None, :, :, 1].astype(jnp.float32)
    coil_image = jnp.stack(
        [map_re * image_re - map_im * image_im, map_re * image_im + map_im * image_re], axis=3
    ).astype(jnp.bfloat16)
    partly = jnp.einsum(
        "pqky,tcsqyx->tcspkx", section_one, coil_image, preferred_element_type=jnp.float32
    ).astype(jnp.bfloat16)
    spectra = jnp.einsum(
        "tcsqyx,qpkx->tcspyk", partly, section_two, preferred_element_type=jnp.float32
    )
    phase_angle = slice_phases(shift_index, phase_offset, matrix)
    cosine = jnp.cos(phase_angle)[None, None, :, :, None]
    sine = jnp.sin(phase_angle)[None, None, :, :, None]
    spec_re = spectra[:, :, :, 0]
    spec_im = spectra[:, :, :, 1]
    shifted = jnp.stack(
        [spec_re * cosine - spec_im * sine, spec_re * sine + spec_im * cosine], axis=3
    ).astype(jnp.bfloat16)
    position = lax.axis_index("slc")
    within = jnp.arange(per_device, dtype=jnp.int32)
    classes = (position * per_device + within) % groups
    class_match = (classes[:, None] == jnp.arange(groups, dtype=jnp.int32)[None, :]).astype(
        jnp.int32
    )
    target = jnp.sum(class_match * group_order[None, :], axis=1)
    slot_index = target * spread + within // groups
    onehot = (jnp.arange(slot_count, dtype=jnp.int32)[:, None] == slot_index[None, :]).astype(
        jnp.int32
    )
    source = jnp.sum(onehot * within[None, :], axis=1)
    filled = jnp.sum(onehot, axis=1)
    outgoing = jnp.take(shifted, source, axis=2)
    outgoing = jnp.where(
        filled[None, None, :, None, None, None] > 0, outgoing, jnp.zeros_like(outgoing)
    )
    incoming = lax.all_to_all(outgoing, "slc", split_axis=2, concat_axis=2, tiled=True)
    aliased = jnp.sum(incoming, axis=2, dtype=jnp.float32)
    residual = (aliased - kspace[:, 0].astype(jnp.float32)).astype(jnp.bfloat16)
    partial_value = jnp.einsum(
        "tcpyx,tcyx->py",
        incoming[:, :, :, 0],
        residual[:, :, 1],
        preferred_element_type=jnp.float32,
    )
    partial_value = partial_value - jnp.einsum(
        "tcpyx,tcyx->py",
        incoming[:, :, :, 1],
        residual[:, :, 0],
        preferred_element_type=jnp.float32,
    )
    returned = lax.all_to_all(partial_value, "slc", split_axis=0, concat_axis=0, tiled=True)
    local_grad = jnp.dot(onehot.T.astype(jnp.float32), returned, precision=lax.Precision.HIGHEST)
    summed = lax.psum(local_grad, "coil")
    summed = lax.psum(summed, "vol")
    factor = 1.0 / (
        coil_maps.shape[0] * lax.axis_size("coil") * images.shape[0] * lax.axis_size("vol")
    )
    return summed * factor


def solution(mesh):
    placed = (
        P(("grp", "vol"), "slc", None, None, None),
        P(("grp", "coil"), "slc", None, None, None),
        P(("grp", "vol"), "slc", "coil", None, None, None),
        P("slc"),
        P("slc", None),
        P(),
    )
    return jax.shard_map(
        program, mesh=mesh, in_specs=placed, out_specs=P(("grp", "slc"), None), check_vma=False
    )
```
